256 devices in a mesh: grid: 64 (over y_hi, x, z), freq: 4 (over y_lo, core).
Axes of the slice: x: 4, y: 4 (y_hi: 2, y_lo: 2; y = y_hi * 2 + y_lo), z: 8, core: 2. Of those that a mesh axis runs over, the one named last changes fastest.
Arguments:
- traces: bfloat16 [256, 64, 16, 2048], P(('grid', 'freq')), may hold values from -6 to 6
- bins: int32 [256, 64, 16], P(('grid', 'freq')), may hold values from 0 to 12287, as said below
- live: int32 [256, 64, 16], P(('grid', 'freq')), may hold values 0 or 1
- probe: float32 [64, 2, 24], replicated, may hold values from -0.5 to 0.5
Outputs:
- reconstructed: float32 [768, 16, 64, 512], P('grid', None, None, 'freq')
The draws below stay inside these ranges and needn't reach their ends.
Inputs may be any that keep to these rules, and one draw needn't show every extreme that they name: Within one destination tile the bins of all sources' slots are distinct; in each tile some slot names cell 0 and some slot names cell 12288 - 1.
All inputs are finite; a program needn't handle non-finite values. No bound on the sum of `live` on one device may be relied on, other than what follows from the above.
Results may differ from the reference program's by a relative error of at most 0.0052.
Values may be sent and summed in bfloat16 or wider, within the bound.
A program may use at most 128 MiB of HBM per device.

```python
import math
import jax
import jax.numpy as jnp
from jax import lax

NT = 2048
FDEV = 64
FIRST = 8
RANK = 24
PX = 16
MY = 16
HX = 8
HY = 8
MARGIN = 2
SLOT = 16
OWNX = 12
NF = 256
NSRC = 256
CELLS = 12288
N_GRID = 64
N_FREQ = 4


def draw_bins(key, part):
    incoming = NSRC * SLOT

    def one_tile(patch_random_key):
        leading_seed = jax.random.fold_in(patch_random_key, 11)
        second_random_key = jax.random.fold_in(patch_random_key, 12)
        central_part = jax.random.permutation(leading_seed, CELLS - 2).astype(jnp.int32) + 1
        chosen = jnp.concatenate([jnp.array([CELLS - 1, 0], dtype=jnp.int32), central_part[:incoming - 2]])
        order = jax.random.permutation(second_random_key, incoming)
        return chosen[order].reshape(NSRC, SLOT)
    tile_keys = jax.vmap(lambda index: jax.random.fold_in(key, index))(jnp.arange(N_GRID, dtype=jnp.int32))
    per_tile = jax.vmap(one_tile)(tile_keys)
    return jnp.transpose(per_tile, (1, 0, 2)).astype(jnp.int32)


def plant(drawn, stream_key, smallest, top_value):
    longest = drawn.shape.index(max(drawn.shape))
    spots = []
    for shift in (0, 1):
        where = [jax.random.randint(jax.random.fold_in(stream_key, axis), (), 0, length) for axis, length in enumerate(drawn.shape)]
        where[longest] = (where[longest] + shift) % drawn.shape[longest]
        spots.append(tuple(where))
    return drawn.at[spots[0]].set(smallest).at[spots[1]].set(top_value)


def block_scale(rng, dims, split, low, largest):
    factor_of = 1.0
    for dim, shards_of in split:
        steps = jax.random.uniform(jax.random.fold_in(jax.random.fold_in(rng, 6), dim), (shards_of,), jnp.float32, low / len(split), largest / len(split))
        factor_of = factor_of * jnp.repeat(jnp.exp(steps), dims[dim] // shards_of).reshape((-1,) + (1,) * (len(dims) - 1 - dim))
    return factor_of


def scatter_about(own_key, shape, spread, most, cuts=(), kind=jnp.bfloat16):
    gain = block_scale(own_key, shape, cuts, -0.22, 0.18) if cuts else 1.0
    values = jax.random.normal(own_key, shape, jnp.float32) * spread * gain
    return jnp.minimum(jnp.maximum(values, -most), most).astype(kind)


def setup_inputs(seed: int = 0) -> dict:
    splits = jax.random.split(jax.random.key(seed), 5)
    return {
        "traces": scatter_about(splits[0], (NSRC, N_GRID, SLOT, NT), 1.0, 6.0, ((0, 256),)),
        "bins": draw_bins(jax.random.fold_in(splits[4], 71), 0),
        "live": plant((jax.random.randint(splits[2], (NSRC, N_GRID, SLOT), 0, 4) < 3).astype(jnp.int32), jax.random.fold_in(splits[2], 1), 0, 1),
        "probe": scatter_about(splits[3], (HX * HY, 2, RANK), (2 * HX * HY) ** -0.5, 0.5, (), jnp.float32),
    }


def spectral_table(recording_readings, fdev, band_count, first):
    clock_moments = jnp.arange(recording_readings, dtype=jnp.int32)[:, None]
    matrix_field = jnp.arange(2 * fdev * band_count, dtype=jnp.int32)[None, :]
    band_idx = matrix_field // (2 * fdev)
    half_idx = matrix_field // fdev % 2
    offset = matrix_field % fdev
    spectral_bin_number = first + band_idx * fdev + offset
    cycle_rotations = (clock_moments * spectral_bin_number % recording_readings).astype(jnp.float32) * (2.0 * math.pi / recording_readings)
    entries = jnp.where(half_idx == 0, jnp.cos(cycle_rotations), -jnp.sin(cycle_rotations)) / math.sqrt(recording_readings)
    return entries.astype(jnp.bfloat16)

def taper_weights(patch_x, margin):
    position = jnp.arange(patch_x, dtype=jnp.float32)
    ramp = jnp.minimum(position + 1.0, patch_x - position) / (2.0 * margin + 1.0)
    return jnp.minimum(ramp, 1.0)

def reduce_patch(window_record, probe):
    size_x, size_y, offsets, columns = window_record.shape
    fdev = columns // 2
    rank_count = probe.shape[-1]
    highest = lax.Precision.HIGHEST
    patch_rows = window_record.reshape(size_x * size_y, offsets, 2, fdev)
    sketch = jnp.einsum('mhcj,hcr->jmr', patch_rows, probe, precision=highest)
    gram = jnp.einsum('jmr,jms->jrs', sketch, sketch, precision=highest)
    identity = jnp.eye(rank_count, dtype=jnp.float32)
    diag_sum = lax.optimization_barrier(jnp.sum(gram * identity, axis=(1, 2)))
    gram = gram + (0.01 * diag_sum / rank_count + 1e-06)[:, None, None] * identity
    lower_factor = jnp.linalg.cholesky(gram)
    projected = jnp.einsum('jmr,mhcj->jrhc', sketch, patch_rows, precision=highest)
    projected = projected.reshape(fdev, rank_count, offsets * 2)
    inner = lax.linalg.triangular_solve(lower_factor, projected, left_side=True, lower=True)
    coeff = lax.linalg.triangular_solve(lower_factor, inner, left_side=True, lower=True, transpose_a=True)
    coeff = coeff.reshape(fdev, rank_count, offsets, 2)
    rebuilt = jnp.einsum('jmr,jrhc->mhcj', sketch, coeff, precision=highest)
    return rebuilt.reshape(size_x, size_y, offsets, columns)

def reference(traces, bins, live, probe):
    table = spectral_table(NT, FDEV, N_FREQ, FIRST)
    spectra = jnp.dot(traces.reshape(-1, NT).astype(jnp.float32), table.astype(jnp.float32), preferred_element_type=jnp.float32).astype(jnp.bfloat16)
    tile_ids = jnp.arange(N_GRID, dtype=jnp.int32)[None, :, None]
    flat_cells = jnp.where(live == 1, tile_ids * CELLS + bins, N_GRID * CELLS).astype(jnp.int32).reshape(-1)
    binned = jnp.zeros((N_GRID * CELLS, 2 * NF), jnp.bfloat16).at[flat_cells].set(spectra, mode='drop')
    binned = binned.reshape(N_GRID * OWNX, MY, HX * HY, 2 * NF)
    weights = taper_weights(PX, MARGIN)[:, None, None, None]

    def one_band(band_idx):
        band_data = lax.dynamic_slice_in_dim(binned, band_idx * 2 * FDEV, 2 * FDEV, 3)
        padded = jnp.pad(band_data, ((MARGIN, MARGIN), (0, 0), (0, 0), (0, 0)))

        def one_tile(block_number):
            window_record = lax.dynamic_slice_in_dim(padded, block_number * OWNX, PX, 0).astype(jnp.float32)
            return reduce_patch(window_record, probe) * weights
        pieces = lax.map(one_tile, jnp.arange(N_GRID, dtype=jnp.int32))
        core_part = pieces[:, MARGIN:PX - MARGIN]
        core_part = core_part.at[1:, :MARGIN].add(pieces[:-1, PX - MARGIN:])
        core_part = core_part.at[:-1, OWNX - MARGIN:].add(pieces[1:, :MARGIN])
        return core_part.reshape(N_GRID * OWNX, MY, HX * HY, 2 * FDEV)
    bands = lax.map(one_band, jnp.arange(N_FREQ, dtype=jnp.int32))
    return jnp.moveaxis(bands, 0, 3).reshape(N_GRID * OWNX, MY, HX * HY, 2 * NF)
```

```python
import math

import jax
import jax.numpy as jnp
from jax import lax
from jax.experimental import pallas as pl
from jax.experimental.pallas import tpu as pltpu
from jax.sharding import PartitionSpec as P

FDEV = 64
FIRST = 8
PX = 16
MY = 16
HX = 8
HY = 8
MARGIN = 2
OWNX = 12


def extended(cells, sides, width):
    for axis, dim in sides:
        count = lax.axis_size(axis)
        ends = count - 1
        head = lax.slice_in_dim(cells, 0, width, axis=dim)
        tail = lax.slice_in_dim(cells, cells.shape[dim] - width, cells.shape[dim], axis=dim)
        cells = jnp.concatenate(
            [
                lax.ppermute(tail, axis, [(i, (i + 1) % count) for i in range(ends)]),
                cells,
                lax.ppermute(head, axis, [((i + 1) % count, i) for i in range(ends)]),
            ],
            axis=dim,
        )
    return cells


def spectral_table(recording_readings, fdev, band_count, first):
    clock_moments = jnp.arange(recording_readings, dtype=jnp.int32)[:, None]
    matrix_field = jnp.arange(2 * fdev * band_count, dtype=jnp.int32)[None, :]
    band_idx = matrix_field // (2 * fdev)
    half_idx = matrix_field // fdev % 2
    offset = matrix_field % fdev
    spectral_bin_number = first + band_idx * fdev + offset
    cycle_rotations = (clock_moments * spectral_bin_number % recording_readings).astype(
        jnp.float32
    ) * (2.0 * math.pi / recording_readings)
    entries = jnp.where(
        half_idx == 0, jnp.cos(cycle_rotations), -jnp.sin(cycle_rotations)
    ) / math.sqrt(recording_readings)
    return entries.astype(jnp.bfloat16)


def taper_weights(patch_x, margin):
    position = jnp.arange(patch_x, dtype=jnp.float32)
    ramp = jnp.minimum(position + 1.0, patch_x - position) / (2.0 * margin + 1.0)
    return jnp.minimum(ramp, 1.0)


def gram_inverse_kernel(g_ref, o_ref):
    n = g_ref.shape[0]
    rows = [g_ref[r] for r in range(n)]
    diag = rows[0][0:1, :]
    for r in range(1, n):
        diag = diag + rows[r][r : r + 1, :]
    shift = 0.01 * diag / n + 1e-06
    index = lax.broadcasted_iota(jnp.int32, rows[0].shape, 0)
    rows = [rows[r] + jnp.where(index == r, shift, 0.0) for r in range(n)]
    cols = []
    inv_diag = []
    for k in range(n):
        inv = 1.0 / jnp.sqrt(rows[k][k : k + 1, :])
        col = jnp.where(index >= k, rows[k] * inv, 0.0)
        for r in range(k + 1, n):
            rows[r] = rows[r] - col[r : r + 1, :] * col
        cols.append(col)
        inv_diag.append(inv)
    xs = []
    for i in range(n):
        acc = jnp.where(index == i, 1.0, 0.0)
        for p in range(i):
            acc = acc - cols[p][i : i + 1, :] * xs[p]
        xs.append(acc * inv_diag[i])
    for a in range(n):
        total = xs[a][a : a + 1, :] * xs[a]
        for i in range(a + 1, n):
            total = total + xs[i][a : a + 1, :] * xs[i]
        o_ref[a] = total
    return


def gram_inverse(gram):
    return pl.pallas_call(
        gram_inverse_kernel,
        out_shape=jax.ShapeDtypeStruct(gram.shape, jnp.float32),
        in_specs=[pl.BlockSpec(memory_space=pltpu.VMEM)],
        out_specs=pl.BlockSpec(memory_space=pltpu.VMEM),
    )(gram)


def reduce_patch(window_record, probe):
    size_x, size_y, offsets, columns = window_record.shape
    fdev = columns // 2
    highest = lax.Precision.HIGHEST
    patch_rows = window_record.reshape(size_x * size_y, offsets, 2, fdev)
    sketch = jnp.einsum("mhcj,hcr->jmr", patch_rows, probe, precision=highest)
    gram = jnp.einsum("jmr,jms->rsj", sketch, sketch, precision=highest)
    ginv = gram_inverse(gram)
    projected = jnp.einsum("jmr,mhcj->jrhc", sketch, patch_rows, precision=highest)
    coeff = jnp.einsum("rsj,jshc->jrhc", ginv, projected, precision=highest)
    rebuilt = jnp.einsum("jmr,jrhc->mhcj", sketch, coeff, precision=highest)
    return rebuilt.reshape(size_x, size_y, offsets, columns)


def per_device(traces, bins, live, probe):
    grid_count = lax.axis_size("grid")
    freq_count = lax.axis_size("freq")
    slot_count = traces.shape[2]
    recording_readings = traces.shape[3]
    table = lax.optimization_barrier(
        spectral_table(recording_readings, FDEV, freq_count, FIRST)
    )
    spectra = jnp.dot(
        traces.reshape(grid_count * slot_count, recording_readings),
        table,
        preferred_element_type=jnp.float32,
    ).astype(jnp.bfloat16)
    spectra = spectra.reshape(grid_count, slot_count, freq_count, 2 * FDEV)
    plane = MY * HX * HY
    cell_count = OWNX * plane
    my_bins = bins[0]
    is_live = live[0] == 1
    target = jnp.where(is_live, my_bins, cell_count)
    targets = jnp.broadcast_to(target[:, :, None], (grid_count, target.shape[1], freq_count))
    arrived_spectra, arrived_cells = (
        lax.all_to_all(
            lax.all_to_all(spectra, "grid", split_axis=0, concat_axis=0, tiled=True),
            "freq",
            split_axis=2,
            concat_axis=1,
            tiled=True,
        ),
        lax.all_to_all(
            lax.all_to_all(targets, "grid", split_axis=0, concat_axis=0, tiled=True),
            "freq",
            split_axis=2,
            concat_axis=1,
            tiled=True,
        ),
    )
    filled = (
        jnp.zeros((cell_count, 2 * FDEV), jnp.bfloat16)
        .at[arrived_cells.reshape(-1)]
        .set(arrived_spectra.reshape(-1, 2 * FDEV), mode="drop")
    )
    owned_cells = filled.reshape(OWNX, MY, HX * HY, 2 * FDEV)
    window_record = extended(owned_cells, (("grid", 0),), MARGIN)
    weighted = (
        reduce_patch(window_record.astype(jnp.float32), probe)
        * taper_weights(PX, MARGIN)[:, None, None, None]
    )
    core_part = weighted[MARGIN : PX - MARGIN]
    outgoing = jnp.concatenate([weighted[:MARGIN], weighted[PX - MARGIN :]], 0)
    incoming = extended(outgoing, (("grid", 0),), MARGIN)
    from_left = incoming[:MARGIN]
    right_neighbour_rims = incoming[3 * MARGIN :]
    core_part = core_part.at[:MARGIN].add(from_left)
    core_part = core_part.at[OWNX - MARGIN :].add(right_neighbour_rims)
    return core_part


def solution(mesh):
    placed = (
        P(("grid", "freq"), None, None, None),
        P(("grid", "freq"), None, None),
        P(("grid", "freq"), None, None),
        P(),
    )
    return jax.shard_map(
        per_device,
        mesh=mesh,
        in_specs=placed,
        out_specs=P("grid", None, None, "freq"),
        check_vma=False,
    )
```

```python
import math

import jax
import jax.numpy as jnp
from jax import lax
from jax.experimental import pallas as pl
from jax.experimental.pallas import tpu as pltpu
from jax.sharding import PartitionSpec as P

FDEV = 64
FIRST = 8
PX = 16
MY = 16
HX = 8
HY = 8
MARGIN = 2
OWNX = 12


def extended(cells, sides, width):
    for axis, dim in sides:
        count = lax.axis_size(axis)
        ends = count - 1
        head = lax.slice_in_dim(cells, 0, width, axis=dim)
        tail = lax.slice_in_dim(cells, cells.shape[dim] - width, cells.shape[dim], axis=dim)
        cells = jnp.concatenate(
            [
                lax.ppermute(tail, axis, [(i, (i + 1) % count) for i in range(ends)]),
                cells,
                lax.ppermute(head, axis, [((i + 1) % count, i) for i in range(ends)]),
            ],
            axis=dim,
        )
    return cells


def spectral_table(recording_readings, fdev, band_count, first):
    inner = 64
    outer = recording_readings // inner
    matrix_field = jnp.arange(2 * fdev * band_count, dtype=jnp.int32)[None, :]
    band_idx = matrix_field // (2 * fdev)
    half_idx = matrix_field // fdev % 2
    offset = matrix_field % fdev
    spectral_bin_number = first + band_idx * fdev + offset
    step = 2.0 * math.pi / recording_readings

    def angles(moments):
        turns = moments * spectral_bin_number % recording_readings
        return turns.astype(jnp.float32) * step

    high = angles(jnp.arange(outer, dtype=jnp.int32)[:, None] * inner)
    low = angles(jnp.arange(inner, dtype=jnp.int32)[:, None])
    cos_h, sin_h = jnp.cos(high)[:, None, :], jnp.sin(high)[:, None, :]
    cos_l, sin_l = jnp.cos(low)[None, :, :], jnp.sin(low)[None, :, :]
    cosine = cos_h * cos_l - sin_h * sin_l
    sine = sin_h * cos_l + cos_h * sin_l
    entries = jnp.where(half_idx[None] == 0, cosine, -sine) / math.sqrt(recording_readings)
    return entries.reshape(recording_readings, -1).astype(jnp.bfloat16)


def taper_weights(patch_x, margin):
    position = jnp.arange(patch_x, dtype=jnp.float32)
    ramp = jnp.minimum(position + 1.0, patch_x - position) / (2.0 * margin + 1.0)
    return jnp.minimum(ramp, 1.0)


def gram_inverse_kernel(g_ref, o_ref):
    n = g_ref.shape[0]
    rows = [g_ref[r] for r in range(n)]
    diag = rows[0][0:1, :]
    for r in range(1, n):
        diag = diag + rows[r][r : r + 1, :]
    shift = 0.01 * diag / n + 1e-06
    index = lax.broadcasted_iota(jnp.int32, rows[0].shape, 0)
    rows = [rows[r] + jnp.where(index == r, shift, 0.0) for r in range(n)]
    cols = []
    inv_diag = []
    for k in range(n):
        inv = 1.0 / jnp.sqrt(rows[k][k : k + 1, :])
        col = jnp.where(index >= k, rows[k] * inv, 0.0)
        for r in range(k + 1, n):
            rows[r] = rows[r] - col[r : r + 1, :] * col
        cols.append(col)
        inv_diag.append(inv)
    xs = []
    for i in range(n):
        acc = jnp.where(index == i, 1.0, 0.0)
        for p in range(i):
            acc = acc - cols[p][i : i + 1, :] * xs[p]
        xs.append(acc * inv_diag[i])
    for a in range(n):
        total = xs[a][a : a + 1, :] * xs[a]
        for i in range(a + 1, n):
            total = total + xs[i][a : a + 1, :] * xs[i]
        o_ref[a] = total
    return


def gram_inverse(gram):
    return pl.pallas_call(
        gram_inverse_kernel,
        out_shape=jax.ShapeDtypeStruct(gram.shape, jnp.float32),
        in_specs=[pl.BlockSpec(memory_space=pltpu.VMEM)],
        out_specs=pl.BlockSpec(memory_space=pltpu.VMEM),
    )(gram)


def reduce_patch(window_record, probe):
    size_x, size_y, offsets, columns = window_record.shape
    fdev = columns // 2
    highest = lax.Precision.HIGHEST
    patch_rows = window_record.reshape(size_x * size_y, offsets, 2, fdev)
    sketch = jnp.einsum("mhcj,hcr->jmr", patch_rows, probe, precision=highest)
    gram = jnp.einsum("jmr,jms->rsj", sketch, sketch, precision=highest)
    ginv = gram_inverse(gram)
    projected = jnp.einsum("jmr,mhcj->jrhc", sketch, patch_rows, precision=highest)
    coeff = jnp.einsum("rsj,jshc->jrhc", ginv, projected, precision=highest)
    rebuilt = jnp.einsum("jmr,jrhc->mhcj", sketch, coeff, precision=highest)
    return rebuilt.reshape(size_x, size_y, offsets, columns)


def per_device(traces, bins, live, probe):
    grid_count = lax.axis_size("grid")
    freq_count = lax.axis_size("freq")
    slot_count = traces.shape[2]
    recording_readings = traces.shape[3]
    table = lax.optimization_barrier(
        spectral_table(recording_readings, FDEV, freq_count, FIRST)
    )
    spectra = jnp.dot(
        traces.reshape(grid_count * slot_count, recording_readings),
        table,
        preferred_element_type=jnp.float32,
    ).astype(jnp.bfloat16)
    spectra = spectra.reshape(grid_count, slot_count, freq_count, 2 * FDEV)
    spectra = jnp.transpose(spectra, (0, 2, 1, 3)).reshape(
        grid_count * freq_count, slot_count, 2 * FDEV
    )
    plane = MY * HX * HY
    cell_count = OWNX * plane
    my_bins = bins[0]
    is_live = live[0] == 1
    target = jnp.where(is_live, my_bins, cell_count)
    targets = jnp.broadcast_to(
        target[:, None, :], (grid_count, freq_count, target.shape[1])
    ).reshape(grid_count * freq_count, target.shape[1])
    both = ("grid", "freq")
    arrived_spectra = lax.all_to_all(spectra, both, 0, 0, tiled=True)
    arrived_cells = lax.all_to_all(targets, both, 0, 0, tiled=True)
    filled = (
        jnp.zeros((cell_count, 2 * FDEV), jnp.bfloat16)
        .at[arrived_cells.reshape(-1)]
        .set(arrived_spectra.reshape(-1, 2 * FDEV), mode="drop")
    )
    owned_cells = filled.reshape(OWNX, MY, HX * HY, 2 * FDEV)
    window_record = extended(owned_cells, (("grid", 0),), MARGIN)
    weighted = (
        reduce_patch(window_record.astype(jnp.float32), probe)
        * taper_weights(PX, MARGIN)[:, None, None, None]
    )
    core_part = weighted[MARGIN : PX - MARGIN]
    outgoing = jnp.concatenate([weighted[:MARGIN], weighted[PX - MARGIN :]], 0)
    incoming = extended(outgoing.astype(jnp.bfloat16), (("grid", 0),), MARGIN)
    incoming = incoming.astype(jnp.float32)
    from_left = incoming[:MARGIN]
    right_neighbour_rims = incoming[3 * MARGIN :]
    core_part = core_part.at[:MARGIN].add(from_left)
    core_part = core_part.at[OWNX - MARGIN :].add(right_neighbour_rims)
    return core_part


def solution(mesh):
    placed = (
        P(("grid", "freq"), None, None, None),
        P(("grid", "freq"), None, None),
        P(("grid", "freq"), None, None),
        P(),
    )
    return jax.shard_map(
        per_device,
        mesh=mesh,
        in_specs=placed,
        out_specs=P("grid", None, None, "freq"),
        check_vma=False,
    )
```

```python
import math

import jax
import jax.numpy as jnp
from jax import lax
from jax.experimental import pallas as pl
from jax.experimental.pallas import tpu as pltpu
from jax.sharding import PartitionSpec as P

FDEV = 64
FIRST = 8
PX = 16
MY = 16
HX = 8
HY = 8
MARGIN = 2
OWNX = 12


def extended(cells, sides, width):
    for axis, dim in sides:
        count = lax.axis_size(axis)
        ends = count - 1
        head = lax.slice_in_dim(cells, 0, width, axis=dim)
        tail = lax.slice_in_dim(cells, cells.shape[dim] - width, cells.shape[dim], axis=dim)
        cells = jnp.concatenate(
            [
                lax.ppermute(tail, axis, [(i, (i + 1) % count) for i in range(ends)]),
                cells,
                lax.ppermute(head, axis, [((i + 1) % count, i) for i in range(ends)]),
            ],
            axis=dim,
        )
    return cells


def spectral_table(recording_readings, fdev, band_count, first):
    inner = 64
    outer = recording_readings // inner
    matrix_field = jnp.arange(2 * fdev * band_count, dtype=jnp.int32)[None, :]
    band_idx = matrix_field // (2 * fdev)
    half_idx = matrix_field // fdev % 2
    offset = matrix_field % fdev
    spectral_bin_number = first + band_idx * fdev + offset
    step = 2.0 * math.pi / recording_readings

    def angles(moments):
        turns = moments * spectral_bin_number % recording_readings
        return turns.astype(jnp.float32) * step

    high = angles(jnp.arange(outer, dtype=jnp.int32)[:, None] * inner)
    low = angles(jnp.arange(inner, dtype=jnp.int32)[:, None])
    cos_h, sin_h = jnp.cos(high)[:, None, :], jnp.sin(high)[:, None, :]
    cos_l, sin_l = jnp.cos(low)[None, :, :], jnp.sin(low)[None, :, :]
    cosine = cos_h * cos_l - sin_h * sin_l
    sine = sin_h * cos_l + cos_h * sin_l
    entries = jnp.where(half_idx[None] == 0, cosine, -sine) / math.sqrt(recording_readings)
    return entries.reshape(recording_readings, -1).astype(jnp.bfloat16)


def taper_weights(patch_x, margin):
    position = jnp.arange(patch_x, dtype=jnp.float32)
    ramp = jnp.minimum(position + 1.0, patch_x - position) / (2.0 * margin + 1.0)
    return jnp.minimum(ramp, 1.0)


def gram_inverse_kernel(g_ref, o_ref):
    n = g_ref.shape[0]
    rows = [g_ref[r] for r in range(n)]
    diag = rows[0][0:1, :]
    for r in range(1, n):
        diag = diag + rows[r][r : r + 1, :]
    shift = 0.01 * diag / n + 1e-06
    index = lax.broadcasted_iota(jnp.int32, rows[0].shape, 0)
    rows = [rows[r] + jnp.where(index == r, shift, 0.0) for r in range(n)]
    cols = []
    inv_diag = []
    for k in range(n):
        inv = 1.0 / jnp.sqrt(rows[k][k : k + 1, :])
        col = jnp.where(index >= k, rows[k] * inv, 0.0)
        for r in range(k + 1, n):
            rows[r] = rows[r] - col[r : r + 1, :] * col
        cols.append(col)
        inv_diag.append(inv)
    xs = []
    for i in range(n):
        acc = jnp.where(index == i, 1.0, 0.0)
        for p in range(i):
            acc = acc - cols[p][i : i + 1, :] * xs[p]
        xs.append(acc * inv_diag[i])
    for a in range(n):
        total = xs[a][a : a + 1, :] * xs[a]
        for i in range(a + 1, n):
            total = total + xs[i][a : a + 1, :] * xs[i]
        o_ref[a] = total
    return


def gram_inverse(gram):
    return pl.pallas_call(
        gram_inverse_kernel,
        out_shape=jax.ShapeDtypeStruct(gram.shape, jnp.float32),
        in_specs=[pl.BlockSpec(memory_space=pltpu.VMEM)],
        out_specs=pl.BlockSpec(memory_space=pltpu.VMEM),
    )(gram)


def reduce_patch(window_record, probe):
    size_x, size_y, offsets, columns = window_record.shape
    fdev = columns // 2
    highest = lax.Precision.HIGHEST
    rows = window_record.reshape(size_x * size_y, offsets, columns)
    lane_major = jnp.transpose(rows, (2, 0, 1)).astype(jnp.float32)
    probe_lanes = jnp.broadcast_to(
        jnp.transpose(probe, (1, 0, 2))[:, None], (2, fdev) + (offsets, probe.shape[-1])
    ).reshape(columns, offsets, probe.shape[-1])
    halves = jnp.einsum("lmh,lhr->lmr", lane_major, probe_lanes, precision=highest)
    sketch = halves[:fdev] + halves[fdev:]
    gram = jnp.einsum("jmr,jms->rsj", sketch, sketch, precision=highest)
    ginv = gram_inverse(gram)
    sketch_lanes = jnp.concatenate([sketch, sketch], 0)
    projected = jnp.einsum("lmr,lmh->lrh", sketch_lanes, lane_major, precision=highest)
    ginv_lanes = jnp.concatenate([ginv, ginv], 2)
    coeff = jnp.einsum("rsl,lsh->lrh", ginv_lanes, projected, precision=highest)
    rebuilt = jnp.einsum("lmr,lrh->mhl", sketch_lanes, coeff, precision=highest)
    return rebuilt.reshape(size_x, size_y, offsets, columns)


def per_device(traces, bins, live, probe):
    grid_count = lax.axis_size("grid")
    freq_count = lax.axis_size("freq")
    slot_count = traces.shape[2]
    recording_readings = traces.shape[3]
    table = lax.optimization_barrier(
        spectral_table(recording_readings, FDEV, freq_count, FIRST)
    )
    spectra = jnp.dot(
        traces.reshape(grid_count * slot_count, recording_readings),
        table,
        preferred_element_type=jnp.float32,
    ).astype(jnp.bfloat16)
    spectra = spectra.reshape(grid_count, slot_count, freq_count, 2 * FDEV)
    spectra = jnp.transpose(spectra, (0, 2, 1, 3)).reshape(
        grid_count * freq_count, slot_count, 2 * FDEV
    )
    plane = MY * HX * HY
    cell_count = OWNX * plane
    my_bins = bins[0]
    is_live = live[0] == 1
    target = jnp.where(is_live, my_bins, cell_count)
    targets = jnp.broadcast_to(
        target[:, None, :], (grid_count, freq_count, target.shape[1])
    ).reshape(grid_count * freq_count, target.shape[1])
    both = ("grid", "freq")
    arrived_spectra = lax.all_to_all(spectra, both, 0, 0, tiled=True)
    arrived_cells = lax.all_to_all(targets, both, 0, 0, tiled=True)
    filled = (
        jnp.zeros((cell_count, 2 * FDEV), jnp.bfloat16)
        .at[arrived_cells.reshape(-1)]
        .set(arrived_spectra.reshape(-1, 2 * FDEV), mode="drop")
    )
    owned_cells = filled.reshape(OWNX, MY, HX * HY, 2 * FDEV)
    window_record = extended(owned_cells, (("grid", 0),), MARGIN)
    weighted = (
        reduce_patch(window_record, probe)
        * taper_weights(PX, MARGIN)[:, None, None, None]
    )
    core_part = weighted[MARGIN : PX - MARGIN]
    outgoing = jnp.concatenate([weighted[:MARGIN], weighted[PX - MARGIN :]], 0)
    incoming = extended(outgoing.astype(jnp.bfloat16), (("grid", 0),), MARGIN)
    incoming = incoming.astype(jnp.float32)
    from_left = incoming[:MARGIN]
    right_neighbour_rims = incoming[3 * MARGIN :]
    core_part = core_part.at[:MARGIN].add(from_left)
    core_part = core_part.at[OWNX - MARGIN :].add(right_neighbour_rims)
    return core_part


def solution(mesh):
    placed = (
        P(("grid", "freq"), None, None, None),
        P(("grid", "freq"), None, None),
        P(("grid", "freq"), None, None),
        P(),
    )
    return jax.shard_map(
        per_device,
        mesh=mesh,
        in_specs=placed,
        out_specs=P("grid", None, None, "freq"),
        check_vma=False,
    )
```

```python
import math

import jax
import jax.numpy as jnp
from jax import lax
from jax.experimental import pallas as pl
from jax.experimental.pallas import tpu as pltpu
from jax.sharding import PartitionSpec as P

FDEV = 64
FIRST = 8
PX = 16
MY = 16
HX = 8
HY = 8
MARGIN = 2
OWNX = 12


def extended(cells, sides, width):
    for axis, dim in sides:
        count = lax.axis_size(axis)
        ends = count - 1
        head = lax.slice_in_dim(cells, 0, width, axis=dim)
        tail = lax.slice_in_dim(cells, cells.shape[dim] - width, cells.shape[dim], axis=dim)
        cells = jnp.concatenate(
            [
                lax.ppermute(tail, axis, [(i, (i + 1) % count) for i in range(ends)]),
                cells,
                lax.ppermute(head, axis, [((i + 1) % count, i) for i in range(ends)]),
            ],
            axis=dim,
        )
    return cells


def spectral_table(recording_readings, fdev, band_count, first):
    inner = 64
    outer = recording_readings // inner
    matrix_field = jnp.arange(2 * fdev * band_count, dtype=jnp.int32)[None, :]
    band_idx = matrix_field // (2 * fdev)
    half_idx = matrix_field // fdev % 2
    offset = matrix_field % fdev
    spectral_bin_number = first + band_idx * fdev + offset
    step = 2.0 * math.pi / recording_readings

    def angles(moments):
        turns = moments * spectral_bin_number % recording_readings
        return turns.astype(jnp.float32) * step

    high = angles(jnp.arange(outer, dtype=jnp.int32)[:, None] * inner)
    low = angles(jnp.arange(inner, dtype=jnp.int32)[:, None])
    cos_h, sin_h = jnp.cos(high)[:, None, :], jnp.sin(high)[:, None, :]
    cos_l, sin_l = jnp.cos(low)[None, :, :], jnp.sin(low)[None, :, :]
    cosine = cos_h * cos_l - sin_h * sin_l
    sine = sin_h * cos_l + cos_h * sin_l
    entries = jnp.where(half_idx[None] == 0, cosine, -sine) / math.sqrt(recording_readings)
    return entries.reshape(recording_readings, -1).astype(jnp.bfloat16)


def taper_weights(patch_x, margin):
    position = jnp.arange(patch_x, dtype=jnp.float32)
    ramp = jnp.minimum(position + 1.0, patch_x - position) / (2.0 * margin + 1.0)
    return jnp.minimum(ramp, 1.0)


def gram_inverse_kernel(g_ref, o_ref):
    n = g_ref.shape[0]
    rows = [g_ref[r] for r in range(n)]
    diag = rows[0][0:1, :]
    for r in range(1, n):
        diag = diag + rows[r][r : r + 1, :]
    shift = 0.01 * diag / n + 1e-06
    index = lax.broadcasted_iota(jnp.int32, rows[0].shape, 0)
    rows = [rows[r] + jnp.where(index == r, shift, 0.0) for r in range(n)]
    cols = []
    inv_diag = []
    for k in range(n):
        inv = 1.0 / jnp.sqrt(rows[k][k : k + 1, :])
        col = jnp.where(index >= k, rows[k] * inv, 0.0)
        for r in range(k + 1, n):
            rows[r] = rows[r] - col[r : r + 1, :] * col
        cols.append(col)
        inv_diag.append(inv)
    xs = []
    for i in range(n):
        acc = jnp.where(index == i, 1.0, 0.0)
        for p in range(i):
            acc = acc - cols[p][i : i + 1, :] * xs[p]
        xs.append(acc * inv_diag[i])
    for a in range(n):
        total = xs[a][a : a + 1, :] * xs[a]
        for i in range(a + 1, n):
            total = total + xs[i][a : a + 1, :] * xs[i]
        o_ref[a] = total
    return


def gram_inverse(gram):
    return pl.pallas_call(
        gram_inverse_kernel,
        out_shape=jax.ShapeDtypeStruct(gram.shape, jnp.float32),
        in_specs=[pl.BlockSpec(memory_space=pltpu.VMEM)],
        out_specs=pl.BlockSpec(memory_space=pltpu.VMEM),
    )(gram)


def reduce_patch(window_record, probe):
    size_x, size_y, offsets, columns = window_record.shape
    fdev = columns // 2
    highest = lax.Precision.HIGHEST
    rows = window_record.reshape(size_x * size_y, offsets, columns)
    lane_major = jnp.transpose(rows, (2, 0, 1)).astype(jnp.float32)
    probe_lanes = jnp.broadcast_to(
        jnp.transpose(probe, (1, 0, 2))[:, None], (2, fdev) + (offsets, probe.shape[-1])
    ).reshape(columns, offsets, probe.shape[-1])
    halves = jnp.einsum("lmh,lhr->lmr", lane_major, probe_lanes, precision=highest)
    sketch = halves[:fdev] + halves[fdev:]
    gram = jnp.einsum("jmr,jms->rsj", sketch, sketch, precision=highest)
    ginv = gram_inverse(gram)
    sketch_lanes = jnp.concatenate([sketch, sketch], 0)
    projected = jnp.einsum("lmr,lmh->lrh", sketch_lanes, lane_major, precision=highest)
    ginv_lanes = jnp.concatenate([ginv, ginv], 2)
    coeff = jnp.einsum("rsl,lsh->lrh", ginv_lanes, projected, precision=highest)
    return sketch_lanes, coeff


def rebuild(sketch_lanes, coeff, first, last, size_y):
    highest = lax.Precision.HIGHEST
    part = sketch_lanes[:, first * size_y : last * size_y]
    rebuilt = jnp.einsum("lmr,lrh->mhl", part, coeff, precision=highest)
    weights = taper_weights(PX, MARGIN)[first:last, None, None, None]
    return rebuilt.reshape((last - first, size_y) + rebuilt.shape[1:]) * weights


def per_device(traces, bins, live, probe):
    grid_count = lax.axis_size("grid")
    freq_count = lax.axis_size("freq")
    slot_count = traces.shape[2]
    recording_readings = traces.shape[3]
    table = lax.optimization_barrier(
        spectral_table(recording_readings, FDEV, freq_count, FIRST)
    )
    spectra = jnp.dot(
        traces.reshape(grid_count * slot_count, recording_readings),
        table,
        preferred_element_type=jnp.float32,
    ).astype(jnp.bfloat16)
    spectra = spectra.reshape(grid_count, slot_count, freq_count, 2 * FDEV)
    spectra = jnp.transpose(spectra, (0, 2, 1, 3)).reshape(
        grid_count * freq_count, slot_count, 2 * FDEV
    )
    plane = MY * HX * HY
    cell_count = OWNX * plane
    my_bins = bins[0]
    is_live = live[0] == 1
    target = jnp.where(is_live, my_bins, cell_count)
    targets = jnp.broadcast_to(
        target[:, None, :], (grid_count, freq_count, target.shape[1])
    ).reshape(grid_count * freq_count, target.shape[1])
    both = ("grid", "freq")
    arrived_spectra = lax.all_to_all(spectra, both, 0, 0, tiled=True)
    arrived_cells = lax.all_to_all(targets, both, 0, 0, tiled=True)
    filled = (
        jnp.zeros((cell_count, 2 * FDEV), jnp.bfloat16)
        .at[arrived_cells.reshape(-1)]
        .set(arrived_spectra.reshape(-1, 2 * FDEV), mode="drop")
    )
    owned_cells = filled.reshape(OWNX, MY, HX * HY, 2 * FDEV)
    window_record = extended(owned_cells, (("grid", 0),), MARGIN)
    sketch_lanes, coeff = reduce_patch(window_record, probe)
    outgoing = jnp.concatenate(
        [
            rebuild(sketch_lanes, coeff, 0, MARGIN, MY),
            rebuild(sketch_lanes, coeff, PX - MARGIN, PX, MY),
        ],
        0,
    )
    incoming = extended(outgoing.astype(jnp.bfloat16), (("grid", 0),), MARGIN)
    incoming = incoming.astype(jnp.float32)
    core_part = rebuild(sketch_lanes, coeff, MARGIN, PX - MARGIN, MY)
    from_left = incoming[:MARGIN]
    right_neighbour_rims = incoming[3 * MARGIN :]
    core_part = core_part.at[:MARGIN].add(from_left)
    core_part = core_part.at[OWNX - MARGIN :].add(right_neighbour_rims)
    return core_part


def solution(mesh):
    placed = (
        P(("grid", "freq"), None, None, None),
        P(("grid", "freq"), None, None),
        P(("grid", "freq"), None, None),
        P(),
    )
    return jax.shard_map(
        per_device,
        mesh=mesh,
        in_specs=placed,
        out_specs=P("grid", None, None, "freq"),
        check_vma=False,
    )
```

```python
import math

import jax
import jax.numpy as jnp
from jax import lax
from jax.experimental import pallas as pl
from jax.experimental.pallas import tpu as pltpu
from jax.sharding import PartitionSpec as P

FDEV = 64
FIRST = 8
PX = 16
MY = 16
HX = 8
HY = 8
MARGIN = 2
OWNX = 12


def extended(cells, sides, width):
    for axis, dim in sides:
        count = lax.axis_size(axis)
        ends = count - 1
        head = lax.slice_in_dim(cells, 0, width, axis=dim)
        tail = lax.slice_in_dim(cells, cells.shape[dim] - width, cells.shape[dim], axis=dim)
        cells = jnp.concatenate(
            [
                lax.ppermute(tail, axis, [(i, (i + 1) % count) for i in range(ends)]),
                cells,
                lax.ppermute(head, axis, [((i + 1) % count, i) for i in range(ends)]),
            ],
            axis=dim,
        )
    return cells


def spectral_table(recording_readings, fdev, band_count, first):
    inner = 64
    outer = recording_readings // inner
    matrix_field = jnp.arange(2 * fdev * band_count, dtype=jnp.int32)[None, :]
    band_idx = matrix_field // (2 * fdev)
    half_idx = matrix_field // fdev % 2
    offset = matrix_field % fdev
    spectral_bin_number = first + band_idx * fdev + offset
    step = 2.0 * math.pi / recording_readings

    def angles(moments):
        turns = moments * spectral_bin_number % recording_readings
        return turns.astype(jnp.float32) * step

    high = angles(jnp.arange(outer, dtype=jnp.int32)[:, None] * inner)
    low = angles(jnp.arange(inner, dtype=jnp.int32)[:, None])
    cos_h, sin_h = jnp.cos(high)[:, None, :], jnp.sin(high)[:, None, :]
    cos_l, sin_l = jnp.cos(low)[None, :, :], jnp.sin(low)[None, :, :]
    cosine = cos_h * cos_l - sin_h * sin_l
    sine = sin_h * cos_l + cos_h * sin_l
    entries = jnp.where(half_idx[None] == 0, cosine, -sine) / math.sqrt(recording_readings)
    return entries.reshape(recording_readings, -1).astype(jnp.bfloat16)


def taper_weights(patch_x, margin):
    position = jnp.arange(patch_x, dtype=jnp.float32)
    ramp = jnp.minimum(position + 1.0, patch_x - position) / (2.0 * margin + 1.0)
    return jnp.minimum(ramp, 1.0)


def gram_inverse_kernel(g_ref, o_ref):
    n = g_ref.shape[0]
    rows = [g_ref[r] for r in range(n)]
    diag = rows[0][0:1, :]
    for r in range(1, n):
        diag = diag + rows[r][r : r + 1, :]
    shift = 0.01 * diag / n + 1e-06
    index = lax.broadcasted_iota(jnp.int32, rows[0].shape, 0)
    rows = [rows[r] + jnp.where(index == r, shift, 0.0) for r in range(n)]
    cols = []
    inv_diag = []
    for k in range(n):
        inv = 1.0 / jnp.sqrt(rows[k][k : k + 1, :])
        col = jnp.where(index >= k, rows[k] * inv, 0.0)
        for r in range(k + 1, n):
            rows[r] = rows[r] - col[r : r + 1, :] * col
        cols.append(col)
        inv_diag.append(inv)
    xs = []
    for i in range(n):
        acc = jnp.where(index == i, 1.0, 0.0)
        for p in range(i):
            acc = acc - cols[p][i : i + 1, :] * xs[p]
        xs.append(acc * inv_diag[i])
    for a in range(n):
        total = xs[a][a : a + 1, :] * xs[a]
        for i in range(a + 1, n):
            total = total + xs[i][a : a + 1, :] * xs[i]
        o_ref[a] = total
    return


def gram_inverse(gram):
    return pl.pallas_call(
        gram_inverse_kernel,
        out_shape=jax.ShapeDtypeStruct(gram.shape, jnp.float32),
        in_specs=[pl.BlockSpec(memory_space=pltpu.VMEM)],
        out_specs=pl.BlockSpec(memory_space=pltpu.VMEM),
    )(gram)


def reduce_patch(window_record, probe):
    size_x, size_y, offsets, columns = window_record.shape
    fdev = columns // 2
    highest = lax.Precision.HIGHEST
    rows = window_record.reshape(size_x * size_y, offsets, columns)
    lane_major = jnp.transpose(rows, (2, 0, 1)).astype(jnp.float32)
    probe_lanes = jnp.broadcast_to(
        jnp.transpose(probe, (1, 0, 2))[:, None], (2, fdev) + (offsets, probe.shape[-1])
    ).reshape(columns, offsets, probe.shape[-1])
    halves = jnp.einsum("lmh,lhr->lmr", lane_major, probe_lanes, precision=highest)
    sketch = halves[:fdev] + halves[fdev:]
    gram = jnp.einsum("jmr,jms->rsj", sketch, sketch, precision=highest)
    ginv = gram_inverse(gram)
    sketch_lanes = jnp.concatenate([sketch, sketch], 0)
    projected = jnp.einsum("lmr,lmh->lrh", sketch_lanes, lane_major, precision=highest)
    ginv_lanes = jnp.concatenate([ginv, ginv], 2)
    coeff = jnp.einsum("rsl,lsh->lrh", ginv_lanes, projected, precision=highest)
    rebuilt = jnp.einsum("lmr,lrh->mhl", sketch_lanes, coeff, precision=highest)
    return rebuilt.reshape(size_x, size_y, offsets, columns)


def per_device(traces, bins, live, probe):
    grid_count = lax.axis_size("grid")
    freq_count = lax.axis_size("freq")
    slot_count = traces.shape[2]
    recording_readings = traces.shape[3]
    table = lax.optimization_barrier(
        spectral_table(recording_readings, FDEV, freq_count, FIRST)
    )
    spectra = jnp.dot(
        traces.reshape(grid_count * slot_count, recording_readings),
        table,
        preferred_element_type=jnp.float32,
    ).astype(jnp.bfloat16)
    spectra = spectra.reshape(grid_count, slot_count, freq_count, 2 * FDEV)
    spectra = jnp.transpose(spectra, (0, 2, 1, 3)).reshape(
        grid_count * freq_count, slot_count * 2 * FDEV
    )
    plane = MY * HX * HY
    cell_count = OWNX * plane
    my_bins = bins[0]
    is_live = live[0] == 1
    target = jnp.where(is_live, my_bins, cell_count)
    lanes = 2 * FDEV
    coded = jnp.concatenate(
        [target // lanes, target % lanes], axis=1
    ).astype(jnp.bfloat16)
    coded = jnp.pad(coded, ((0, 0), (0, lanes - coded.shape[1])))
    coded = jnp.broadcast_to(
        coded[:, None, :], (grid_count, freq_count, lanes)
    ).reshape(grid_count * freq_count, lanes)
    payload = jnp.concatenate([spectra, coded], axis=1)
    arrived = lax.all_to_all(payload, ("grid", "freq"), 0, 0, tiled=True)
    arrived_spectra = arrived[:, : slot_count * lanes]
    high = arrived[:, slot_count * lanes : slot_count * lanes + slot_count]
    low = arrived[:, slot_count * lanes + slot_count : slot_count * lanes + 2 * slot_count]
    arrived_cells = high.astype(jnp.int32) * lanes + low.astype(jnp.int32)
    filled = (
        jnp.zeros((cell_count, 2 * FDEV), jnp.bfloat16)
        .at[arrived_cells.reshape(-1)]
        .set(arrived_spectra.reshape(-1, 2 * FDEV), mode="drop")
    )
    owned_cells = filled.reshape(OWNX, MY, HX * HY, 2 * FDEV)
    window_record = extended(owned_cells, (("grid", 0),), MARGIN)
    weighted = (
        reduce_patch(window_record, probe)
        * taper_weights(PX, MARGIN)[:, None, None, None]
    )
    core_part = weighted[MARGIN : PX - MARGIN]
    outgoing = jnp.concatenate([weighted[:MARGIN], weighted[PX - MARGIN :]], 0)
    incoming = extended(outgoing.astype(jnp.bfloat16), (("grid", 0),), MARGIN)
    incoming = incoming.astype(jnp.float32)
    from_left = incoming[:MARGIN]
    right_neighbour_rims = incoming[3 * MARGIN :]
    core_part = core_part.at[:MARGIN].add(from_left)
    core_part = core_part.at[OWNX - MARGIN :].add(right_neighbour_rims)
    return core_part


def solution(mesh):
    placed = (
        P(("grid", "freq"), None, None, None),
        P(("grid", "freq"), None, None),
        P(("grid", "freq"), None, None),
        P(),
    )
    return jax.shard_map(
        per_device,
        mesh=mesh,
        in_specs=placed,
        out_specs=P("grid", None, None, "freq"),
        check_vma=False,
    )
```

```python
import math

import jax
import jax.numpy as jnp
from jax import lax
from jax.experimental import pallas as pl
from jax.experimental.pallas import tpu as pltpu
from jax.sharding import PartitionSpec as P

FDEV = 64
FIRST = 8
PX = 16
MY = 16
HX = 8
HY = 8
MARGIN = 2
OWNX = 12


def extended(cells, sides, width):
    for axis, dim in sides:
        count = lax.axis_size(axis)
        ends = count - 1
        head = lax.slice_in_dim(cells, 0, width, axis=dim)
        tail = lax.slice_in_dim(cells, cells.shape[dim] - width, cells.shape[dim], axis=dim)
        cells = jnp.concatenate(
            [
                lax.ppermute(tail, axis, [(i, (i + 1) % count) for i in range(ends)]),
                cells,
                lax.ppermute(head, axis, [((i + 1) % count, i) for i in range(ends)]),
            ],
            axis=dim,
        )
    return cells


def spectral_table(recording_readings, fdev, band_count, first):
    inner = 64
    outer = recording_readings // inner
    matrix_field = jnp.arange(2 * fdev * band_count, dtype=jnp.int32)[None, :]
    band_idx = matrix_field // (2 * fdev)
    half_idx = matrix_field // fdev % 2
    offset = matrix_field % fdev
    spectral_bin_number = first + band_idx * fdev + offset
    step = 2.0 * math.pi / recording_readings

    def angles(moments):
        turns = moments * spectral_bin_number % recording_readings
        return turns.astype(jnp.float32) * step

    high = angles(jnp.arange(outer, dtype=jnp.int32)[:, None] * inner)
    low = angles(jnp.arange(inner, dtype=jnp.int32)[:, None])
    cos_h, sin_h = jnp.cos(high)[:, None, :], jnp.sin(high)[:, None, :]
    cos_l, sin_l = jnp.cos(low)[None, :, :], jnp.sin(low)[None, :, :]
    cosine = cos_h * cos_l - sin_h * sin_l
    sine = sin_h * cos_l + cos_h * sin_l
    entries = jnp.where(half_idx[None] == 0, cosine, -sine) / math.sqrt(recording_readings)
    return entries.reshape(recording_readings, -1).astype(jnp.bfloat16)


def taper_weights(patch_x, margin):
    position = jnp.arange(patch_x, dtype=jnp.float32)
    ramp = jnp.minimum(position + 1.0, patch_x - position) / (2.0 * margin + 1.0)
    return jnp.minimum(ramp, 1.0)


def gram_inverse_kernel(g_ref, o_ref):
    n = g_ref.shape[0]
    rows = [g_ref[r] for r in range(n)]
    diag = rows[0][0:1, :]
    for r in range(1, n):
        diag = diag + rows[r][r : r + 1, :]
    shift = 0.01 * diag / n + 1e-06
    index = lax.broadcasted_iota(jnp.int32, rows[0].shape, 0)
    rows = [rows[r] + jnp.where(index == r, shift, 0.0) for r in range(n)]
    cols = []
    inv_diag = []
    for k in range(n):
        inv = 1.0 / jnp.sqrt(rows[k][k : k + 1, :])
        col = jnp.where(index >= k, rows[k] * inv, 0.0)
        for r in range(k + 1, n):
            rows[r] = rows[r] - col[r : r + 1, :] * col
        cols.append(col)
        inv_diag.append(inv)
    xs = []
    for i in range(n):
        acc = jnp.where(index == i, 1.0, 0.0)
        for p in range(i):
            acc = acc - cols[p][i : i + 1, :] * xs[p]
        xs.append(acc * inv_diag[i])
    for a in range(n):
        total = xs[a][a : a + 1, :] * xs[a]
        for i in range(a + 1, n):
            total = total + xs[i][a : a + 1, :] * xs[i]
        o_ref[a] = total
    return


def gram_inverse(gram):
    return pl.pallas_call(
        gram_inverse_kernel,
        out_shape=jax.ShapeDtypeStruct(gram.shape, jnp.float32),
        in_specs=[pl.BlockSpec(memory_space=pltpu.VMEM)],
        out_specs=pl.BlockSpec(memory_space=pltpu.VMEM),
    )(gram)


def reduce_patch(window_record, probe):
    size_x, size_y, offsets, columns = window_record.shape
    fdev = columns // 2
    highest = lax.Precision.HIGHEST
    rows = window_record.reshape(size_x * size_y, offsets, columns)
    lane_major = jnp.transpose(rows, (2, 0, 1)).astype(jnp.float32)
    probe_lanes = jnp.broadcast_to(
        jnp.transpose(probe, (1, 0, 2))[:, None], (2, fdev) + (offsets, probe.shape[-1])
    ).reshape(columns, offsets, probe.shape[-1])
    halves = jnp.einsum("lmh,lhr->lmr", lane_major, probe_lanes, precision=highest)
    sketch = halves[:fdev] + halves[fdev:]
    gram = jnp.einsum("jmr,jms->rsj", sketch, sketch, precision=highest)
    ginv = gram_inverse(gram)
    sketch_lanes = jnp.concatenate([sketch, sketch], 0)
    projected = jnp.einsum("lmr,lmh->lrh", sketch_lanes, lane_major, precision=highest)
    ginv_lanes = jnp.concatenate([ginv, ginv], 2)
    coeff = jnp.einsum("rsl,lsh->lrh", ginv_lanes, projected, precision=highest)
    row_weights = jnp.repeat(taper_weights(size_x, MARGIN), size_y)[None, :, None]
    rebuilt = jnp.einsum(
        "lmr,lrh->mhl", sketch_lanes * row_weights, coeff, precision=highest
    )
    return rebuilt.reshape(size_x, size_y, offsets, columns)


def per_device(traces, bins, live, probe):
    grid_count = lax.axis_size("grid")
    freq_count = lax.axis_size("freq")
    slot_count = traces.shape[2]
    recording_readings = traces.shape[3]
    table = lax.optimization_barrier(
        spectral_table(recording_readings, FDEV, freq_count, FIRST)
    )
    spectra = jnp.dot(
        traces.reshape(grid_count * slot_count, recording_readings),
        table,
        preferred_element_type=jnp.float32,
    ).astype(jnp.bfloat16)
    spectra = spectra.reshape(grid_count, slot_count, freq_count, 2 * FDEV)
    spectra = jnp.transpose(spectra, (0, 2, 1, 3)).reshape(
        grid_count * freq_count, slot_count * 2 * FDEV
    )
    plane = MY * HX * HY
    cell_count = OWNX * plane
    my_bins = bins[0]
    is_live = live[0] == 1
    target = jnp.where(is_live, my_bins, cell_count)
    lanes = 2 * FDEV
    coded = jnp.concatenate(
        [target // lanes, target % lanes], axis=1
    ).astype(jnp.bfloat16)
    coded = jnp.pad(coded, ((0, 0), (0, lanes - coded.shape[1])))
    coded = jnp.broadcast_to(
        coded[:, None, :], (grid_count, freq_count, lanes)
    ).reshape(grid_count * freq_count, lanes)
    payload = jnp.concatenate([spectra, coded], axis=1)
    arrived = lax.all_to_all(payload, ("grid", "freq"), 0, 0, tiled=True)
    arrived_spectra = arrived[:, : slot_count * lanes]
    high = arrived[:, slot_count * lanes : slot_count * lanes + slot_count]
    low = arrived[:, slot_count * lanes + slot_count : slot_count * lanes + 2 * slot_count]
    arrived_cells = high.astype(jnp.int32) * lanes + low.astype(jnp.int32)
    filled = (
        jnp.zeros((cell_count, 2 * FDEV), jnp.bfloat16)
        .at[arrived_cells.reshape(-1)]
        .set(arrived_spectra.reshape(-1, 2 * FDEV), mode="drop")
    )
    owned_cells = filled.reshape(OWNX, MY, HX * HY, 2 * FDEV)
    window_record = extended(owned_cells, (("grid", 0),), MARGIN)
    weighted = reduce_patch(window_record, probe)
    core_part = weighted[MARGIN : PX - MARGIN]
    outgoing = jnp.concatenate([weighted[:MARGIN], weighted[PX - MARGIN :]], 0)
    incoming = extended(outgoing.astype(jnp.bfloat16), (("grid", 0),), MARGIN)
    incoming = incoming.astype(jnp.float32)
    from_left = incoming[:MARGIN]
    right_neighbour_rims = incoming[3 * MARGIN :]
    core_part = core_part.at[:MARGIN].add(from_left)
    core_part = core_part.at[OWNX - MARGIN :].add(right_neighbour_rims)
    return core_part


def solution(mesh):
    placed = (
        P(("grid", "freq"), None, None, None),
        P(("grid", "freq"), None, None),
        P(("grid", "freq"), None, None),
        P(),
    )
    return jax.shard_map(
        per_device,
        mesh=mesh,
        in_specs=placed,
        out_specs=P("grid", None, None, "freq"),
        check_vma=False,
    )
```

```python
import math

import jax
import jax.numpy as jnp
from jax import lax
from jax.experimental import pallas as pl
from jax.experimental.pallas import tpu as pltpu
from jax.sharding import PartitionSpec as P

FDEV = 64
FIRST = 8
PX = 16
MY = 16
HX = 8
HY = 8
MARGIN = 2
OWNX = 12


def extended(cells, sides, width):
    for axis, dim in sides:
        count = lax.axis_size(axis)
        ends = count - 1
        head = lax.slice_in_dim(cells, 0, width, axis=dim)
        tail = lax.slice_in_dim(cells, cells.shape[dim] - width, cells.shape[dim], axis=dim)
        cells = jnp.concatenate(
            [
                lax.ppermute(tail, axis, [(i, (i + 1) % count) for i in range(ends)]),
                cells,
                lax.ppermute(head, axis, [((i + 1) % count, i) for i in range(ends)]),
            ],
            axis=dim,
        )
    return cells


def spectral_table(recording_readings, fdev, band_count, first):
    inner = 64
    outer = recording_readings // inner
    matrix_field = jnp.arange(2 * fdev * band_count, dtype=jnp.int32)[None, :]
    band_idx = matrix_field // (2 * fdev)
    half_idx = matrix_field // fdev % 2
    offset = matrix_field % fdev
    spectral_bin_number = first + band_idx * fdev + offset
    step = 2.0 * math.pi / recording_readings

    def angles(moments):
        turns = moments * spectral_bin_number % recording_readings
        return turns.astype(jnp.float32) * step

    high = angles(jnp.arange(outer, dtype=jnp.int32)[:, None] * inner)
    low = angles(jnp.arange(inner, dtype=jnp.int32)[:, None])
    cos_h, sin_h = jnp.cos(high)[:, None, :], jnp.sin(high)[:, None, :]
    cos_l, sin_l = jnp.cos(low)[None, :, :], jnp.sin(low)[None, :, :]
    cosine = cos_h * cos_l - sin_h * sin_l
    sine = sin_h * cos_l + cos_h * sin_l
    entries = jnp.where(half_idx[None] == 0, cosine, -sine) / math.sqrt(recording_readings)
    return entries.reshape(recording_readings, -1).astype(jnp.bfloat16)


def taper_weights(patch_x, margin):
    position = jnp.arange(patch_x, dtype=jnp.float32)
    ramp = jnp.minimum(position + 1.0, patch_x - position) / (2.0 * margin + 1.0)
    return jnp.minimum(ramp, 1.0)


def gram_inverse_kernel(g_ref, o_ref):
    n = g_ref.shape[0]
    rows = [g_ref[r] for r in range(n)]
    diag = rows[0][0:1, :]
    for r in range(1, n):
        diag = diag + rows[r][r : r + 1, :]
    shift = 0.01 * diag / n + 1e-06
    index = lax.broadcasted_iota(jnp.int32, rows[0].shape, 0)
    rows = [rows[r] + jnp.where(index == r, shift, 0.0) for r in range(n)]
    cols = []
    inv_diag = []
    for k in range(n):
        inv = 1.0 / jnp.sqrt(rows[k][k : k + 1, :])
        col = jnp.where(index >= k, rows[k] * inv, 0.0)
        for r in range(k + 1, n):
            rows[r] = rows[r] - col[r : r + 1, :] * col
        cols.append(col)
        inv_diag.append(inv)
    xs = []
    for i in range(n):
        acc = jnp.where(index == i, 1.0, 0.0)
        for p in range(i):
            acc = acc - cols[p][i : i + 1, :] * xs[p]
        xs.append(acc * inv_diag[i])
    for a in range(n):
        total = xs[a][a : a + 1, :] * xs[a]
        for i in range(a + 1, n):
            total = total + xs[i][a : a + 1, :] * xs[i]
        o_ref[a] = total
    return


def gram_inverse(gram):
    return pl.pallas_call(
        gram_inverse_kernel,
        out_shape=jax.ShapeDtypeStruct(gram.shape, jnp.float32),
        in_specs=[pl.BlockSpec(memory_space=pltpu.VMEM)],
        out_specs=pl.BlockSpec(memory_space=pltpu.VMEM),
    )(gram)


def reduce_patch(window_record, probe):
    size_x, size_y, offsets, columns = window_record.shape
    fdev = columns // 2
    highest = lax.Precision.HIGHEST
    rows = window_record.reshape(size_x * size_y, offsets, columns)
    lane_major = jnp.transpose(rows, (2, 0, 1)).astype(jnp.float32)
    probe_lanes = jnp.broadcast_to(
        jnp.transpose(probe, (1, 0, 2))[:, None], (2, fdev) + (offsets, probe.shape[-1])
    ).reshape(columns, offsets, probe.shape[-1])
    halves = jnp.einsum("lmh,lhr->lmr", lane_major, probe_lanes, precision=highest)
    sketch = halves[:fdev] + halves[fdev:]
    gram = jnp.einsum("jmr,jms->rsj", sketch, sketch, precision=highest)
    ginv = gram_inverse(gram)
    sketch_lanes = jnp.concatenate([sketch, sketch], 0)
    projected = jnp.einsum("lmr,lmh->lrh", sketch_lanes, lane_major, precision=highest)
    ginv_lanes = jnp.concatenate([ginv, ginv], 2)
    coeff = jnp.einsum("rsl,lsh->lrh", ginv_lanes, projected, precision=highest)
    rebuilt = jnp.einsum("lmr,lrh->mhl", sketch_lanes, coeff, precision=highest)
    return rebuilt.reshape(size_x, size_y, offsets, columns)


def per_device(traces, bins, live, probe):
    grid_count = lax.axis_size("grid")
    freq_count = lax.axis_size("freq")
    slot_count = traces.shape[2]
    recording_readings = traces.shape[3]
    table = lax.optimization_barrier(
        spectral_table(recording_readings, FDEV, freq_count, FIRST)
    )
    spectra = jnp.dot(
        traces.reshape(grid_count * slot_count, recording_readings),
        table,
        preferred_element_type=jnp.float32,
    ).astype(jnp.bfloat16)
    spectra = spectra.reshape(grid_count, slot_count, freq_count, 2 * FDEV)
    spectra = jnp.transpose(spectra, (0, 2, 1, 3)).reshape(
        grid_count * freq_count, slot_count * 2 * FDEV
    )
    plane = MY * HX * HY
    cell_count = OWNX * plane
    my_bins = bins[0]
    is_live = live[0] == 1
    target = jnp.where(is_live, my_bins, cell_count)
    lanes = 2 * FDEV
    coded = jnp.concatenate(
        [target // lanes, target % lanes], axis=1
    ).astype(jnp.bfloat16)
    coded = jnp.pad(coded, ((0, 0), (0, lanes - coded.shape[1])))
    coded = jnp.broadcast_to(
        coded[:, None, :], (grid_count, freq_count, lanes)
    ).reshape(grid_count * freq_count, lanes)
    payload = jnp.concatenate([spectra, coded], axis=1)
    arrived = lax.all_to_all(payload, ("grid", "freq"), 0, 0, tiled=True)
    arrived_spectra = arrived[:, : slot_count * lanes]
    high = arrived[:, slot_count * lanes : slot_count * lanes + slot_count]
    low = arrived[:, slot_count * lanes + slot_count : slot_count * lanes + 2 * slot_count]
    arrived_cells = high.astype(jnp.int32) * lanes + low.astype(jnp.int32)
    flat_cells = arrived_cells.reshape(-1)
    spare = cell_count + jnp.arange(flat_cells.shape[0], dtype=jnp.int32)
    flat_cells = jnp.where(flat_cells < cell_count, flat_cells, spare)
    filled = (
        jnp.zeros((cell_count + flat_cells.shape[0], 2 * FDEV), jnp.bfloat16)
        .at[flat_cells]
        .set(arrived_spectra.reshape(-1, 2 * FDEV), unique_indices=True)
    )[:cell_count]
    owned_cells = filled.reshape(OWNX, MY, HX * HY, 2 * FDEV)
    window_record = extended(owned_cells, (("grid", 0),), MARGIN)
    weighted = (
        reduce_patch(window_record, probe)
        * taper_weights(PX, MARGIN)[:, None, None, None]
    )
    core_part = weighted[MARGIN : PX - MARGIN]
    outgoing = jnp.concatenate([weighted[:MARGIN], weighted[PX - MARGIN :]], 0)
    incoming = extended(outgoing.astype(jnp.bfloat16), (("grid", 0),), MARGIN)
    incoming = incoming.astype(jnp.float32)
    from_left = incoming[:MARGIN]
    right_neighbour_rims = incoming[3 * MARGIN :]
    core_part = core_part.at[:MARGIN].add(from_left)
    core_part = core_part.at[OWNX - MARGIN :].add(right_neighbour_rims)
    return core_part


def solution(mesh):
    placed = (
        P(("grid", "freq"), None, None, None),
        P(("grid", "freq"), None, None),
        P(("grid", "freq"), None, None),
        P(),
    )
    return jax.shard_map(
        per_device,
        mesh=mesh,
        in_specs=placed,
        out_specs=P("grid", None, None, "freq"),
        check_vma=False,
    )
```
